128 devices in a mesh: pipe: 8 (over y, x_lo), seq: 16 (over z, x_hi, core).
Axes of the slice: x: 4 (x_hi: 2, x_lo: 2; x = x_hi * 2 + x_lo), y: 4, z: 4, core: 2. Of those that a mesh axis runs over, the one named last changes fastest.
Arguments:
- held: bfloat16 [8, 2048, 1536], P('pipe', 'seq'), may hold values from -6 to 6
- entering: bfloat16 [2048, 1536], P('seq'), may hold values from -6 to 6
- counts: int32 [9], replicated, may hold values from 1 to 256
- kind: int32 [8], P('pipe'), may hold values from 0 to 1
- modulation: float32 [8, 6, 1536], P('pipe'), may hold values from -4 to 4
- w_qkv: bfloat16 [8, 1536, 6144], P('pipe'), may hold values from -0.15625 to 0.15625
- w_out: bfloat16 [8, 2048, 1536], P('pipe'), may hold values from -0.125 to 0.125
- q_gain: float32 [8, 128], P('pipe'), may hold values from 1.5 to 6
- k_gain: float32 [8, 128], P('pipe'), may hold values from 1.5 to 6
Outputs:
- arrived: bfloat16 [2, 8, 2048, 1536], P(None, 'pipe', 'seq')
The draws below stay inside these ranges and needn't reach their ends.
All inputs are finite; a program needn't handle non-finite values.
Results may differ from the reference program's by a relative error of at most 0.023.
The reference program's roundings to bfloat16 on the way count: a program that leaves them out, or rounds other values in their place, can miss the bound.
Values may be sent and summed in bfloat16 or wider, within the bound.
A program may use at most 128 MiB of HBM per device.

```python
import jax
import jax.numpy as jnp
from jax import lax

D = 1536
HEADS = 16
HD = 128
TXT = 256
INNER = 2048
SECTIONS = 8
SEQ = 2048


def draw_q_gain(key, part):
    key = jax.random.fold_in(key, 101)
    return jax.random.uniform(key, (SECTIONS, HD), jnp.float32, 1.5, 2.5)


def draw_k_gain(key, part):
    key = jax.random.fold_in(key, 202)
    return jax.random.uniform(key, (SECTIONS, HD), jnp.float32, 1.5, 2.5)


def plant(values, rng, least, top_value):
    index_at = [jax.random.randint(jax.random.fold_in(rng, axis), (), 0, length) for axis, length in enumerate(values.shape)]
    main_axis = values.shape.index(max(values.shape))
    neighbour = index_at[:main_axis] + [(index_at[main_axis] + 1) % values.shape[main_axis]] + index_at[main_axis + 1:]
    return values.at[tuple(index_at)].set(least).at[tuple(neighbour)].set(top_value)


def block_levels(rng, dims, cuts, least, top_value):
    level, own = 1.0, jax.random.fold_in(rng, 6)
    for dim, parts in cuts:
        steps = jnp.exp(jax.random.uniform(jax.random.fold_in(own, dim), (parts,), jnp.float32, least / len(cuts), top_value / len(cuts)))
        level = level * jnp.repeat(steps, dims[dim] // parts).reshape([-1 if axis == dim else 1 for axis in range(len(dims))])
    return level


def centred(own_key, extent, scale, bound, pieces=(), kind=jnp.bfloat16):
    result = scale * jax.random.normal(own_key, extent, jnp.float32)
    if pieces:
        result = result * block_levels(own_key, extent, pieces, -0.22, 0.18)
    return jnp.clip(result, -bound, bound).astype(kind)


def setup_inputs(seed: int = 0) -> dict:
    streams_of = jax.random.split(jax.random.key(seed), 10)
    held = centred(streams_of[0], (SECTIONS, SEQ, D), 1.0, 6.0, ((0, 8), (1, 16)))
    entering = centred(streams_of[1], (SEQ, D), 1.0, 6.0, ((0, 16),))
    counts = plant(jax.random.randint(streams_of[2], (SECTIONS + 1,), 1, TXT + 1), jax.random.fold_in(streams_of[2], 1), 1, TXT).astype(jnp.int32)
    kind = plant(jax.random.randint(streams_of[3], (SECTIONS,), 0, 2), jax.random.fold_in(streams_of[3], 1), 0, 1).astype(jnp.int32)
    modulation = centred(streams_of[4], (SECTIONS, 6, D), 1.0, 4.0, ((0, 8),), jnp.float32)
    w_qkv = centred(streams_of[5], (SECTIONS, D, 3 * INNER), D ** -0.5, 0.15625, ((0, 8),))
    w_out = centred(streams_of[6], (SECTIONS, INNER, D), INNER ** -0.5, 0.125, ((0, 8),))
    q_gain = draw_q_gain(jax.random.fold_in(streams_of[9], 71), 0)
    k_gain = draw_k_gain(jax.random.fold_in(streams_of[9], 71), 0)
    return {"held": held, "entering": entering, "counts": counts, "kind": kind, "modulation": modulation, "w_qkv": w_qkv, "w_out": w_out, "q_gain": q_gain, "k_gain": k_gain}


eps = 1e-06

def rms_heads(values_f32, gain):
    return values_f32 * lax.rsqrt(lax.optimization_barrier(jnp.mean(values_f32 * values_f32, axis=-1, keepdims=True)) + eps) * gain

def run_block(resid, section_id, text_live, kind, modulation, w_qkv, w_out, q_gain, k_gain):
    positions = jnp.arange(SEQ, dtype=jnp.int32)
    resid_f32 = resid.astype(jnp.float32)
    center = resid_f32 - lax.optimization_barrier(jnp.mean(resid_f32, axis=-1, keepdims=True))
    normed = center * lax.rsqrt(lax.optimization_barrier(jnp.mean(center * center, axis=-1, keepdims=True)) + eps)
    params = modulation[section_id]
    choose = ((positions >= SEQ - TXT) & (kind[section_id] == 0))[:, None]
    shift_row = jnp.where(choose, params[3], params[0])
    scale_row = jnp.where(choose, params[4], params[1])
    gate_row = jnp.where(choose, params[5], params[2])
    mixed_in = (normed * (1.0 + scale_row) + shift_row).astype(jnp.bfloat16)
    projected = jnp.dot(mixed_in, w_qkv[section_id], preferred_element_type=jnp.float32)
    query_heads = rms_heads(projected[:, :INNER].reshape(SEQ, HEADS, HD), q_gain[section_id]).astype(jnp.bfloat16).transpose(1, 0, 2)
    key_heads = rms_heads(projected[:, INNER:2 * INNER].reshape(SEQ, HEADS, HD), k_gain[section_id]).astype(jnp.bfloat16).transpose(1, 0, 2)
    value_heads = projected[:, 2 * INNER:].reshape(SEQ, HEADS, HD).astype(jnp.bfloat16).transpose(1, 0, 2)
    key_live = positions < SEQ - TXT + text_live

    def attend(head_trio):
        query_one, key_one, value_one = head_trio
        scores = jnp.dot(query_one, key_one.T, preferred_element_type=jnp.float32) * HD ** (-0.5)
        scores = jnp.where(key_live[None, :], scores, -1e+30)
        row_top = lax.optimization_barrier(jnp.max(scores, axis=-1, keepdims=True))
        weights = jnp.exp(scores - row_top)
        denom = lax.optimization_barrier(jnp.sum(weights, axis=-1, keepdims=True))
        summed = jnp.dot(weights.astype(jnp.bfloat16), value_one, preferred_element_type=jnp.float32)
        return (summed / denom).astype(jnp.bfloat16)
    attended = lax.map(attend, (query_heads, key_heads, value_heads))
    merged = attended.transpose(1, 0, 2).reshape(SEQ, INNER)
    update = jnp.dot(merged, w_out[section_id], preferred_element_type=jnp.float32)
    return (resid_f32 + gate_row * update).astype(jnp.bfloat16)

def reference(held, entering, counts, kind, modulation, w_qkv, w_out, q_gain, k_gain):
    section_ids = jnp.arange(SECTIONS, dtype=jnp.int32)

    def first_step(section_id):
        return run_block(held[section_id], section_id, counts[section_id], kind, modulation, w_qkv, w_out, q_gain, k_gain)
    tick_one = lax.map(first_step, section_ids)
    arrived_one = jnp.roll(tick_one, 1, axis=0)
    inputs_two = arrived_one.at[0].set(entering)
    live_two = counts[((section_ids + SECTIONS) % (SECTIONS + 1)).astype(jnp.int32)]

    def second_step(section_id):
        return run_block(inputs_two[section_id], section_id, live_two[section_id], kind, modulation, w_qkv, w_out, q_gain, k_gain)
    tick_two = lax.map(second_step, section_ids)
    arrived_two = jnp.roll(tick_two, 1, axis=0)
    return jnp.stack([arrived_one, arrived_two])
```

```python
import functools

import jax
import jax.numpy as jnp
from jax import lax
from jax.experimental import pallas as pl
from jax.experimental.pallas import tpu as pltpu
from jax.sharding import PartitionSpec as P

HD = 128
TXT = 256
EPS = 1e-06
MESH = pl.DeviceIdType.MESH
LOG2E = 1.4426950408889634

HOPS = (2, 1, 3, 0)


def body(
    counts_ref,
    kind_ref,
    held_hbm,
    entering_hbm,
    mod_ref,
    wqkv_hbm,
    wout_hbm,
    qg_ref,
    kg_ref,
    out_ref,
    w_ref,
    wo_ref,
    xin_ref,
    xother_ref,
    xsend_ref,
    mixed_ref,
    qkv_ref,
    qkvs_ref,
    att_ref,
    atts_ref,
    load_sem,
    w_sem,
    wo_sem,
    cross_send,
    cross_recv,
    qkv_send,
    qkv_recv,
    att_send,
    att_recv,
    pipe_send,
    pipe_recv,
):
    rows, width = xin_ref.shape[1], xin_ref.shape[2]
    inner = wo_ref.shape[0]
    section = lax.axis_index("pipe")
    rank = lax.axis_index("seq")
    sections = lax.axis_size("pipe")
    ranks = lax.axis_size("seq")
    z, xh, core = rank // 4, (rank // 2) % 2, rank % 2
    other = z * 4 + (1 - xh) * 2 + core
    following = (section + 1) % sections
    before = (section + sections - 1) % sections
    seq_total = rows * ranks
    text_start = seq_total - TXT

    barrier = pltpu.get_barrier_semaphore()
    for step in range(1, ranks):
        pl.semaphore_signal(
            barrier, 1, device_id=(section, (rank + step) % ranks), device_id_type=MESH
        )
    for there in (following, before):
        for column in (rank, other):
            pl.semaphore_signal(barrier, 1, device_id=(there, column), device_id_type=MESH)

    loads = [
        pltpu.make_async_copy(held_hbm.at[0], xin_ref.at[0], load_sem.at[0]),
        pltpu.make_async_copy(entering_hbm, xin_ref.at[1], load_sem.at[1]),
    ]
    for copy in loads:
        copy.start()
    weight_loads = []
    for j, hop in enumerate(HOPS):
        for cc in range(2):
            head = ((z + hop) % 4) * 4 + xh * 2 + (core + cc) % 2
            for part in range(3):
                copy = pltpu.make_async_copy(
                    wqkv_hbm.at[
                        0, :, pl.ds(pl.multiple_of(part * inner + head * HD, HD), HD)
                    ],
                    w_ref.at[j, :, pl.ds((part * 2 + cc) * HD, HD)],
                    w_sem.at[j, cc, part],
                )
                copy.start()
                weight_loads.append(copy)
    wo_load = pltpu.make_async_copy(wout_hbm.at[0], wo_ref, wo_sem)
    wo_load.start()

    for copy in loads:
        copy.wait()
    pl.semaphore_wait(barrier, ranks - 1 + 4)

    cross_one = pltpu.make_async_remote_copy(
        xin_ref.at[0],
        xother_ref.at[0],
        cross_send.at[0],
        cross_recv.at[0],
        device_id=(section, other),
        device_id_type=MESH,
    )
    cross_one.start()
    cross_two = pltpu.make_async_remote_copy(
        xin_ref.at[1],
        xother_ref.at[1],
        cross_send.at[1],
        cross_recv.at[1],
        device_id=(section, other),
        device_id_type=MESH,
    )

    @pl.when(section == 0)
    def _():
        cross_two.start()

    kind_row = jnp.full((1, width), kind_ref[0], jnp.int32)

    def mod_row(index, column):
        text = (column >= text_start // rows).astype(jnp.int32)
        pick = (kind_row == 0) & (jnp.full((1, width), text, jnp.int32) == 1)
        return jnp.where(pick, mod_ref[0, index + 3 : index + 4], mod_ref[0, index : index + 1])

    def mix(x, half, column):
        x = x.astype(jnp.float32)
        center = x - jnp.mean(x, axis=-1, keepdims=True)
        normed = center * lax.rsqrt(jnp.mean(center * center, axis=-1, keepdims=True) + EPS)
        mixed = normed * (1.0 + mod_row(1, column)) + mod_row(0, column)
        mixed_ref[half] = mixed.astype(jnp.bfloat16)

    def qkv_copy(step, half, j, cc, column):
        target = ((z + HOPS[j]) % 4) * 4 + xh * 2 + (core + cc) % 2
        return pltpu.make_async_remote_copy(
            qkvs_ref.at[step, half, j, cc],
            qkv_ref.at[step, pl.ds(pl.multiple_of(column * rows, rows), rows), :],
            qkv_send.at[step, half, j, cc],
            qkv_recv.at[step, half, j, cc],
            device_id=(section, target),
            device_id_type=MESH,
        )

    def rms(values, gain):
        return (
            values
            * lax.rsqrt(jnp.mean(values * values, axis=-1, keepdims=True) + EPS)
            * gain
        ).astype(jnp.bfloat16)

    def project(step, half, column):
        for j, hop in enumerate(HOPS):
            if step == 0 and half == 0:
                for copy in weight_loads[j * 6 : (j + 1) * 6]:
                    copy.wait()
            product = jnp.dot(
                mixed_ref[half], w_ref[j], preferred_element_type=jnp.float32
            )
            for cc in range(2):
                query, key, value = (
                    product[:, (part * 2 + cc) * HD : (part * 2 + cc + 1) * HD]
                    for part in range(3)
                )
                query = rms(query, qg_ref[...])
                key = rms(key, kg_ref[...])
                value = value.astype(jnp.bfloat16)
                if hop == 0 and cc == 0:
                    slot = pl.ds(pl.multiple_of(column * rows, rows), rows)
                    qkv_ref[step, slot, 0:HD] = query
                    qkv_ref[step, slot, HD : 2 * HD] = key
                    qkv_ref[step, slot, 2 * HD : 3 * HD] = value
                else:
                    qkvs_ref[step, half, j, cc, :, 0:HD] = query
                    qkvs_ref[step, half, j, cc, :, HD : 2 * HD] = key
                    qkvs_ref[step, half, j, cc, :, 2 * HD : 3 * HD] = value
                    qkv_copy(step, half, j, cc, column).start()

    def remote_pairs():
        return [(j, cc) for j in range(4) for cc in range(2) if HOPS[j] or cc]

    def att_copy(step, i, cc):
        zt = (z + i + 1) % 4
        xt = (xh + 1 - i // 4) % 2
        ct = (core + cc) % 2
        return pltpu.make_async_remote_copy(
            atts_ref.at[step, i, pl.ds(pl.multiple_of(ct * rows, rows), rows), :],
            att_ref.at[step, :, pl.ds(pl.multiple_of(rank * HD, HD), HD)],
            att_send.at[step, i, cc],
            att_recv.at[step, i, cc],
            device_id=(section, zt * 4 + xt * 2 + ct),
            device_id_type=MESH,
        )

    def attend(step, live):
        limit = jnp.full((2 * rows, TXT), text_start + live, jnp.int32)

        def chunk(i, carry):
            zt = (z + i + 1) % 4
            xt = (xh + 1 - i // 4) % 2
            start = pl.multiple_of((zt * 4 + xt * 2) * rows, 2 * rows)
            query = qkv_ref[step, pl.ds(start, 2 * rows), 0:HD]
            scores = lax.dot_general(
                query,
                qkv_ref[step, :, HD : 2 * HD],
                (((1,), (1,)), ((), ())),
                preferred_element_type=jnp.float32,
            )
            place = text_start + lax.broadcasted_iota(jnp.int32, (2 * rows, TXT), 1)
            tail = jnp.where(place < limit, scores[:, text_start:], -1e30)
            scores = jnp.concatenate([scores[:, :text_start], tail], axis=1)
            top = jnp.max(scores, axis=-1, keepdims=True)
            weights = jnp.exp2((scores - top) * (HD ** (-0.5) * LOG2E))
            denom = jnp.sum(weights, axis=-1, keepdims=True)
            summed = jnp.dot(
                weights.astype(jnp.bfloat16),
                qkv_ref[step, :, 2 * HD : 3 * HD],
                preferred_element_type=jnp.float32,
            )
            atts_ref[step, i] = (summed / denom).astype(jnp.bfloat16)

            @pl.when(i < 7)
            def _():
                att_copy(step, i, 0).start()

            att_copy(step, i, 1).start()
            return carry

        lax.fori_loop(0, 8, chunk, 0)
        att_ref[step, :, pl.ds(pl.multiple_of(rank * HD, HD), HD)] = atts_ref[
            step, 7, pl.ds(pl.multiple_of(core * rows, rows), rows), :
        ]

    def finish(step, x):
        gate = mod_row(2, rank)
        tile = 512
        for n in range(width // tile):
            cols = slice(n * tile, (n + 1) * tile)
            update = jnp.dot(
                att_ref[step], wo_ref[:, cols], preferred_element_type=jnp.float32
            )
            xsend_ref[step, :, cols] = (
                x[:, cols].astype(jnp.float32) + gate[:, cols] * update
            ).astype(jnp.bfloat16)

    def pipe_copy(step, column, which):
        return pltpu.make_async_remote_copy(
            xsend_ref.at[step],
            out_ref.at[step] if which == 0 else xother_ref.at[1],
            pipe_send.at[step, which],
            pipe_recv.at[step] if which == 0 else cross_recv.at[1],
            device_id=(following, column),
            device_id_type=MESH,
        )

    mix(xin_ref[0], 0, rank)
    project(0, 0, rank)
    cross_one.wait()
    mix(xother_ref[0], 1, other)
    project(0, 1, other)

    def middle(step, live):
        for half, column in ((0, rank), (1, other)):
            for j, cc in remote_pairs():
                qkv_copy(step, half, j, cc, column).wait_recv()
        attend(step, live)
        for i in range(8):
            for cc in range(2):
                if i < 7 or cc:
                    att_copy(step, i, cc).wait_recv()

    middle(0, counts_ref[section])
    wo_load.wait()
    finish(0, xin_ref[0])
    pipe_copy(0, rank, 0).start()

    @pl.when(section < sections - 1)
    def _():
        pipe_copy(0, other, 1).start()

    pipe_copy(0, rank, 0).wait_recv()

    @pl.when(section > 0)
    def _():
        xin_ref[1] = out_ref[0]

    mix(xin_ref[1], 0, rank)
    project(1, 0, rank)
    cross_two.wait_recv()
    mix(xother_ref[1], 1, other)
    project(1, 1, other)
    middle(1, counts_ref[(section + sections) % (sections + 1)])
    finish(1, xin_ref[1])
    pipe_copy(1, rank, 0).start()

    @pl.when(section == 0)
    def _():
        cross_two.wait_send()

    @pl.when(section < sections - 1)
    def _():
        pipe_copy(0, other, 1).wait_send()

    pipe_copy(0, rank, 0).wait_send()
    for step in range(2):
        for half, column in ((0, rank), (1, other)):
            for j, cc in remote_pairs():
                qkv_copy(step, half, j, cc, column).wait_send()
        for i in range(8):
            for cc in range(2):
                if i < 7 or cc:
                    att_copy(step, i, cc).wait_send()
    pipe_copy(1, rank, 0).wait()


def shards(held, entering, counts, kind, modulation, w_qkv, w_out, q_gain, k_gain):
    rows, width = entering.shape
    inner = w_out.shape[1]
    ranks = lax.axis_size("seq")
    bf16 = jnp.bfloat16
    vmem = pl.BlockSpec(memory_space=pltpu.VMEM)
    smem = pl.BlockSpec(memory_space=pltpu.SMEM)
    hbm = pl.BlockSpec(memory_space=pl.ANY)
    dma = pltpu.SemaphoreType.DMA
    out = pl.pallas_call(
        body,
        out_shape=jax.ShapeDtypeStruct((2, rows, width), bf16),
        in_specs=[smem, smem, hbm, hbm, vmem, hbm, hbm, vmem, vmem],
        out_specs=vmem,
        scratch_shapes=[
            pltpu.VMEM((4, width, 6 * HD), bf16),
            pltpu.VMEM((inner, width), bf16),
            pltpu.VMEM((2, rows, width), bf16),
            pltpu.VMEM((2, rows, width), bf16),
            pltpu.VMEM((2, rows, width), bf16),
            pltpu.VMEM((2, rows, width), bf16),
            pltpu.VMEM((2, rows * ranks, 3 * HD), bf16),
            pltpu.VMEM((2, 2, 4, 2, rows, 3 * HD), bf16),
            pltpu.VMEM((2, rows, inner), bf16),
            pltpu.VMEM((2, 8, 2 * rows, HD), bf16),
            dma((2,)),
            dma((4, 2, 3)),
            dma,
            dma((2,)),
            dma((2,)),
            dma((2, 2, 4, 2)),
            dma((2, 2, 4, 2)),
            dma((2, 8, 2)),
            dma((2, 8, 2)),
            dma((2, 2)),
            dma((2,)),
        ],
        compiler_params=pltpu.CompilerParams(
            collective_id=0, has_side_effects=True, vmem_limit_bytes=60 * 1024 * 1024
        ),
        name="relay",
    )(counts, kind, held, entering, modulation, w_qkv, w_out, q_gain, k_gain)
    return out[:, None]


def solution(mesh):
    placed = (
        P("pipe", "seq", None),
        P("seq", None),
        P(),
        P("pipe"),
        P("pipe", None, None),
        P("pipe", None, None),
        P("pipe", None, None),
        P("pipe", None),
        P("pipe", None),
    )
    return jax.shard_map(
        shards, mesh=mesh, in_specs=placed, out_specs=P(None, "pipe", "seq", None), check_vma=False
    )
```

```python
import functools

import jax
import jax.numpy as jnp
from jax import lax
from jax.experimental import pallas as pl
from jax.experimental.pallas import tpu as pltpu
from jax.sharding import PartitionSpec as P

HD = 128
TXT = 256
EPS = 1e-06
MESH = pl.DeviceIdType.MESH
LOG2E = 1.4426950408889634

HOPS = (2, 1, 3, 0)
PARTS = 4


def body(
    counts_ref,
    kind_ref,
    held_hbm,
    entering_hbm,
    mod_ref,
    wqkv_hbm,
    wout_hbm,
    qg_ref,
    kg_ref,
    out_ref,
    w_ref,
    wo_ref,
    xin_ref,
    xother_ref,
    xsend_ref,
    relay_ref,
    mixed_ref,
    kv_ref,
    q_ref,
    kvs_ref,
    qs_ref,
    att_ref,
    atts_ref,
    load_sem,
    w_sem,
    wo_sem,
    cross_send,
    cross_recv,
    kv_send,
    kv_recv,
    q_send,
    q_recv,
    att_send,
    att_recv,
    pipe_send,
    pipe_recv,
    relay_recv,
    relay_send,
):
    rows, width = xin_ref.shape[1], xin_ref.shape[2]
    half = rows // 2
    part = rows // PARTS
    inner = wo_ref.shape[0]
    section = lax.axis_index("pipe")
    rank = lax.axis_index("seq")
    sections = lax.axis_size("pipe")
    ranks = lax.axis_size("seq")
    z, xh, core = rank // 4, (rank // 2) % 2, rank % 2
    other = z * 4 + (1 - xh) * 2 + core
    place = z * 2 + core
    following = (section + 1) % sections
    before = (section + sections - 1) % sections
    ahead = (section + 2) % sections
    behind = (section + sections - 2) % sections
    odd = section % 2 == 1
    text_start = rows * ranks - TXT

    barrier = pltpu.get_barrier_semaphore()
    for step in range(1, ranks):
        pl.semaphore_signal(
            barrier, 1, device_id=(section, (rank + step) % ranks), device_id_type=MESH
        )
    for there in (following, before):
        for column in (rank, other):
            pl.semaphore_signal(barrier, 1, device_id=(there, column), device_id_type=MESH)
    for there in (ahead, behind):
        pl.semaphore_signal(barrier, 1, device_id=(there, rank), device_id_type=MESH)

    loads = [
        pltpu.make_async_copy(held_hbm.at[0], xin_ref.at[0], load_sem.at[0]),
        pltpu.make_async_copy(entering_hbm, xin_ref.at[1], load_sem.at[1]),
    ]
    for copy in loads:
        copy.start()
    weight_loads = {}
    for hop in HOPS:
        for cc in range(2):
            head = ((z + hop) % 4) * 4 + xh * 2 + (core + cc) % 2
            for third in range(3):
                copy = pltpu.make_async_copy(
                    wqkv_hbm.at[
                        0, :, pl.ds(pl.multiple_of(third * inner + head * HD, HD), HD)
                    ],
                    w_ref.at[hop, :, pl.ds((third * 2 + cc) * HD, HD)],
                    w_sem.at[hop, cc, third],
                )
                copy.start()
                weight_loads.setdefault(hop, []).append(copy)
    wo_load = pltpu.make_async_copy(wout_hbm.at[0], wo_ref, wo_sem)
    wo_load.start()

    for copy in loads:
        copy.wait()
    pl.semaphore_wait(barrier, ranks - 1 + 6)

    def cross_copy(index):
        if index < 2:
            lines = pl.ds(index * half, half)
            source, target = xin_ref.at[0, lines], xother_ref.at[0, lines]
        else:
            source, target = xin_ref.at[1], xother_ref.at[1]
        return pltpu.make_async_remote_copy(
            source,
            target,
            cross_send.at[index],
            cross_recv.at[index],
            device_id=(section, other),
            device_id_type=MESH,
        )

    cross_copy(0).start()
    cross_copy(1).start()

    @pl.when(section == 0)
    def _():
        cross_copy(2).start()

    kind_row = jnp.full((1, width), kind_ref[0], jnp.int32)

    def mod_row(index, column):
        text = (column >= text_start // rows).astype(jnp.int32)
        pick = (kind_row == 0) & (jnp.full((1, width), text, jnp.int32) == 1)
        return jnp.where(pick, mod_ref[0, index + 3 : index + 4], mod_ref[0, index : index + 1])

    def mix(x, start, column):
        x = x.astype(jnp.float32)
        center = x - jnp.mean(x, axis=-1, keepdims=True)
        normed = center * lax.rsqrt(jnp.mean(center * center, axis=-1, keepdims=True) + EPS)
        mixed = normed * (1.0 + mod_row(1, column)) + mod_row(0, column)
        mixed_ref[start : start + x.shape[0]] = mixed.astype(jnp.bfloat16)

    chunks = (
        (0, slice(None), 0),
        (0, 0, 1),
        (0, 1, 1),
        (1, 0, slice(None)),
        (1, 1, slice(None)),
    )

    def pieces(chunk):
        return 1 if chunk in (1, 2) else 2

    def cut(ref, chunk):
        return ref.at[0] if pieces(chunk) == 1 else ref

    def exchange(chunk, hop, cc, keys):
        step, halves, column = chunks[chunk]
        target = ((z + hop) % 4) * 4 + xh * 2 + (core + cc) % 2
        if keys:
            source = cut(kvs_ref.at[chunk, hop, cc], chunk)
            there = kv_ref.at[step, place, halves, column]
            sems = kv_send, kv_recv
        else:
            source = cut(qs_ref.at[chunk, hop, cc], chunk)
            there = q_ref.at[step, halves, place, column]
            sems = q_send, q_recv
        return pltpu.make_async_remote_copy(
            source,
            there,
            sems[0].at[chunk, hop, cc],
            sems[1].at[chunk, hop, cc],
            device_id=(section, target),
            device_id_type=MESH,
        )

    def rms(values, gain):
        return (
            values
            * lax.rsqrt(jnp.mean(values * values, axis=-1, keepdims=True) + EPS)
            * gain
        ).astype(jnp.bfloat16)

    def project(chunk):
        step, halves, column = chunks[chunk]
        count = pieces(chunk)
        shape = (count, half, HD) if count == 2 else (half, HD)
        for hop in HOPS:
            if chunk == 0:
                for copy in weight_loads[hop]:
                    copy.wait()
            product = jnp.dot(
                mixed_ref[0 : count * half], w_ref[hop], preferred_element_type=jnp.float32
            )
            for cc in range(2):
                query, key, value = (
                    product[:, (third * 2 + cc) * HD : (third * 2 + cc + 1) * HD]
                    for third in range(3)
                )
                query = rms(query, qg_ref[...]).reshape(shape)
                key = rms(key, kg_ref[...]).reshape(shape)
                value = value.astype(jnp.bfloat16).reshape(shape)
                if hop == 0 and cc == 0:
                    kv_ref[step, place, halves, column, :, 0:HD] = key
                    kv_ref[step, place, halves, column, :, HD : 2 * HD] = value
                    q_ref[step, halves, place, column] = query
                else:
                    first = slice(None) if count == 2 else 0
                    kvs_ref[chunk, hop, cc, first, :, 0:HD] = key
                    kvs_ref[chunk, hop, cc, first, :, HD : 2 * HD] = value
                    qs_ref[chunk, hop, cc, first] = query
                    exchange(chunk, hop, cc, True).start()

    pairs = [(hop, cc) for hop in (0, 3, 2, 1) for cc in range(2) if hop or cc]

    def send_queries(chunk):
        for hop, cc in pairs:
            exchange(chunk, hop, cc, False).start()

    def att_copy(step, n, column, cc):
        step_z = (n + n // 4) % 4
        at = n // 4
        ct = (core + cc) % 2
        return pltpu.make_async_remote_copy(
            atts_ref.at[step, n, ct, column],
            att_ref.at[
                step,
                pl.ds(pl.multiple_of(at * half, half), half),
                pl.ds(pl.multiple_of(rank * HD, HD), HD),
            ],
            att_send.at[step, at, step_z, column, cc],
            att_recv.at[step, at, step_z, column, cc],
            device_id=(
                section,
                ((z + step_z) % 4) * 4 + ((xh + column) % 2) * 2 + ct,
            ),
            device_id_type=MESH,
        )

    def finish(step, at):
        for n in range(4 * at, 4 * at + 4):
            for column in range(2):
                for cc in range(2):
                    if (n + n // 4) % 4 or column or cc:
                        att_copy(step, n, column, cc).wait_recv()
        gate = mod_row(2, rank)
        lines = slice(at * half, (at + 1) * half)
        tile = 512
        for n in range(width // tile):
            cols = slice(n * tile, (n + 1) * tile)
            update = jnp.dot(
                att_ref[step, lines], wo_ref[:, cols], preferred_element_type=jnp.float32
            )
            xsend_ref[step, lines, cols] = (
                xin_ref[step, lines, cols].astype(jnp.float32) + gate[:, cols] * update
            ).astype(jnp.bfloat16)
        for index in range(at * PARTS // 2, (at + 1) * PARTS // 2):
            if step == 1:
                pipe_copy(1, index).start()
            else:

                @pl.when(odd)
                def _():
                    relay_copy(index).start()

                @pl.when(jnp.logical_not(odd))
                def _():
                    pipe_copy(0, index).start()
                    side_copy(index).start()

    def part_of(index):
        return pl.ds(index * part, part)

    def pipe_copy(step, index):
        return pltpu.make_async_remote_copy(
            xsend_ref.at[step, part_of(index)],
            out_ref.at[step, part_of(index)],
            pipe_send.at[step, index],
            pipe_recv.at[step, index],
            device_id=(following, rank),
            device_id_type=MESH,
        )

    def side_copy(index):
        return pltpu.make_async_remote_copy(
            xsend_ref.at[0, part_of(index)],
            xother_ref.at[1, part_of(index)],
            pipe_send.at[2, index],
            pipe_recv.at[2, index],
            device_id=(following, other),
            device_id_type=MESH,
        )

    def relay_copy(index):
        return pltpu.make_async_remote_copy(
            xsend_ref.at[0, part_of(index)],
            relay_ref.at[part_of(index)],
            pipe_send.at[0, index],
            relay_recv.at[index],
            device_id=(ahead, rank),
            device_id_type=MESH,
        )

    def forward_copy(index, which):
        return pltpu.make_async_remote_copy(
            relay_ref.at[part_of(index)],
            (out_ref.at[0] if which == 0 else xother_ref.at[1]).at[part_of(index)],
            relay_send.at[which, index],
            pipe_recv.at[2 * which, index],
            device_id=(before, rank if which == 0 else other),
            device_id_type=MESH,
        )

    def attend(step, live):
        for chunk in range(5):
            if chunks[chunk][0] == step:
                for hop, cc in pairs:
                    exchange(chunk, hop, cc, True).wait_recv()
        spot = lax.broadcasted_iota(jnp.int32, (1, 4 * rows), 1)
        column = (xh + (spot // half) % 2) % 2
        key_rank = 12 + column * 2 + spot // (2 * rows)
        position = key_rank * rows + ((spot // rows) % 2) * half + spot % half
        limit = jnp.full((1, 4 * rows), text_start + live, jnp.int32)
        bias = jnp.where(position < limit, 0.0, -1e30).astype(jnp.float32)
        clear = (ranks - 4) * rows

        def pair(i, carry):
            @pl.when(i == 3)
            def _():
                if step == 0:
                    wo_load.wait()
                finish(step, 0)

            scores = []
            for u in range(2):
                n = 2 * i + u
                at = n // 4
                step_z = (n + at) % 4
                hop = (4 - step_z) % 4
                for cc in range(2):
                    for chunk in range(5):
                        if chunks[chunk][0] == step:
                            if step == 0:
                                due = at == 0
                            else:
                                due = at == chunk - 3
                            if cc == 0:
                                due = due & (step_z > 0)

                            @pl.when(due)
                            def _():
                                exchange(chunk, hop, cc, False).wait_recv()

                zt = (z + step_z) % 4
                query = q_ref[step, at, pl.ds(2 * zt, 2)].reshape(2 * rows, HD)
                keys = kv_ref[step, :, :, :, :, 0:HD].reshape(ranks * rows, HD)
                scores.append(
                    lax.dot_general(
                        query,
                        keys,
                        (((1,), (1,)), ((), ())),
                        preferred_element_type=jnp.float32,
                    )
                )
            for u in range(2):
                n = 2 * i + u
                at = n // 4
                step_z = (n + at) % 4
                score = jnp.concatenate(
                    [scores[u][:, :clear], scores[u][:, clear:] + bias], axis=1
                )
                top = jnp.max(score, axis=-1, keepdims=True)
                weights = jnp.exp2((score - top) * (HD ** (-0.5) * LOG2E))
                denom = jnp.sum(weights, axis=-1, keepdims=True)
                values = kv_ref[step, :, :, :, :, HD : 2 * HD].reshape(ranks * rows, HD)
                summed = jnp.dot(
                    weights.astype(jnp.bfloat16), values, preferred_element_type=jnp.float32
                )
                atts_ref[step, n] = (
                    (summed / denom).astype(jnp.bfloat16).reshape(2, 2, half, HD)
                )

                @pl.when(step_z > 0)
                def _():
                    att_copy(step, n, 0, 0).start()

                @pl.when(step_z == 0)
                def _():
                    att_ref[
                        step,
                        pl.ds(pl.multiple_of(at * half, half), half),
                        pl.ds(pl.multiple_of(rank * HD, HD), HD),
                    ] = atts_ref[step, n, core, 0]

                att_copy(step, n, 0, 1).start()
                att_copy(step, n, 1, 0).start()
                att_copy(step, n, 1, 1).start()
            return carry

        lax.fori_loop(0, 4, pair, 0)
        finish(step, 1)

    mix(xin_ref[0], 0, rank)
    project(0)
    send_queries(0)
    for at in range(2):
        cross_copy(at).wait_recv()
        mix(xother_ref[0, at * half : (at + 1) * half], 0, other)
        project(1 + at)
    send_queries(1)
    send_queries(2)
    attend(0, counts_ref[section])

    @pl.when(odd)
    def _():
        for index in range(PARTS):
            relay_copy(index).wait_recv()
            forward_copy(index, 0).start()

            @pl.when(section != 1)
            def _():
                forward_copy(index, 1).start()

    for at in range(2):
        lines = slice(at * half, (at + 1) * half)
        for index in range(at * PARTS // 2, (at + 1) * PARTS // 2):
            pipe_copy(0, index).wait_recv()

        @pl.when(section > 0)
        def _():
            xin_ref[1, lines] = out_ref[0, lines]
            for index in range(at * PARTS // 2, (at + 1) * PARTS // 2):
                side_copy(index).wait_recv()

        if at == 0:

            @pl.when(section == 0)
            def _():
                cross_copy(2).wait_recv()

        mix(xin_ref[1, lines], 0, rank)
        mix(xother_ref[1, lines], half, other)
        project(3 + at)
    send_queries(3)
    send_queries(4)
    attend(1, counts_ref[(section + sections) % (sections + 1)])

    cross_copy(0).wait_send()
    cross_copy(1).wait_send()

    @pl.when(section == 0)
    def _():
        cross_copy(2).wait_send()

    @pl.when(jnp.logical_not(odd))
    def _():
        for index in range(PARTS):
            side_copy(index).wait_send()

    @pl.when(odd)
    def _():
        for index in range(PARTS):
            forward_copy(index, 0).wait_send()

            @pl.when(section != 1)
            def _():
                forward_copy(index, 1).wait_send()

    for index in range(PARTS):
        pipe_copy(0, index).wait_send()
    for chunk in range(5):
        for hop, cc in pairs:
            exchange(chunk, hop, cc, True).wait_send()
            exchange(chunk, hop, cc, False).wait_send()
    for step in range(2):
        for n in range(8):
            for column in range(2):
                for cc in range(2):
                    if (n + n // 4) % 4 or column or cc:
                        att_copy(step, n, column, cc).wait_send()
    for index in range(PARTS):
        pipe_copy(1, index).wait()


def shards(held, entering, counts, kind, modulation, w_qkv, w_out, q_gain, k_gain):
    rows, width = entering.shape
    half = rows // 2
    inner = w_out.shape[1]
    bf16 = jnp.bfloat16
    vmem = pl.BlockSpec(memory_space=pltpu.VMEM)
    smem = pl.BlockSpec(memory_space=pltpu.SMEM)
    hbm = pl.BlockSpec(memory_space=pl.ANY)
    dma = pltpu.SemaphoreType.DMA
    out = pl.pallas_call(
        body,
        out_shape=jax.ShapeDtypeStruct((2, rows, width), bf16),
        in_specs=[smem, smem, hbm, hbm, vmem, hbm, hbm, vmem, vmem],
        out_specs=vmem,
        scratch_shapes=[
            pltpu.VMEM((4, width, 6 * HD), bf16),
            pltpu.VMEM((inner, width), bf16),
            pltpu.VMEM((2, rows, width), bf16),
            pltpu.VMEM((2, rows, width), bf16),
            pltpu.VMEM((2, rows, width), bf16),
            pltpu.VMEM((rows, width), bf16),
            pltpu.VMEM((rows, width), bf16),
            pltpu.VMEM((2, 8, 2, 2, half, 2 * HD), bf16),
            pltpu.VMEM((2, 2, 8, 2, half, HD), bf16),
            pltpu.VMEM((5, 4, 2, 2, half, 2 * HD), bf16),
            pltpu.VMEM((5, 4, 2, 2, half, HD), bf16),
            pltpu.VMEM((2, rows, inner), bf16),
            pltpu.VMEM((2, 8, 2, 2, half, HD), bf16),
            dma((2,)),
            dma((4, 2, 3)),
            dma,
            dma((3,)),
            dma((3,)),
            dma((5, 4, 2)),
            dma((5, 4, 2)),
            dma((5, 4, 2)),
            dma((5, 4, 2)),
            dma((2, 2, 4, 2, 2)),
            dma((2, 2, 4, 2, 2)),
            dma((3, PARTS)),
            dma((3, PARTS)),
            dma((PARTS,)),
            dma((2, PARTS)),
        ],
        compiler_params=pltpu.CompilerParams(
            collective_id=0, has_side_effects=True, vmem_limit_bytes=60 * 1024 * 1024
        ),
        name="relay",
    )(counts, kind, held, entering, modulation, w_qkv, w_out, q_gain, k_gain)
    return out[:, None]


def solution(mesh):
    placed = (
        P("pipe", "seq", None),
        P("seq", None),
        P(),
        P("pipe"),
        P("pipe", None, None),
        P("pipe", None, None),
        P("pipe", None, None),
        P("pipe", None),
        P("pipe", None),
    )
    return jax.shard_map(
        shards, mesh=mesh, in_specs=placed, out_specs=P(None, "pipe", "seq", None), check_vma=False
    )
```

```python
import functools

import jax
import jax.numpy as jnp
from jax import lax
from jax.experimental import pallas as pl
from jax.experimental.pallas import tpu as pltpu
from jax.sharding import PartitionSpec as P

HD = 128
TXT = 256
EPS = 1e-06
MESH = pl.DeviceIdType.MESH
LOG2E = 1.4426950408889634

HOPS = (2, 1, 3, 0)
PARTS = 4


def body(
    counts_ref,
    kind_ref,
    held_hbm,
    entering_hbm,
    mod_ref,
    wqkv_hbm,
    wout_hbm,
    qg_ref,
    kg_ref,
    out_ref,
    w_ref,
    wo_ref,
    xin_ref,
    xother_ref,
    xsend_ref,
    relay_ref,
    mixed_ref,
    kv_ref,
    q_ref,
    kvs_ref,
    qs_ref,
    att_ref,
    atts_ref,
    load_sem,
    w_sem,
    wo_sem,
    cross_send,
    cross_recv,
    kv_send,
    kv_recv,
    q_send,
    q_recv,
    att_send,
    att_recv,
    pipe_send,
    pipe_recv,
    relay_recv,
    relay_send,
):
    rows, width = xin_ref.shape[1], xin_ref.shape[2]
    half = rows // 2
    part = rows // PARTS
    inner = wo_ref.shape[0]
    section = lax.axis_index("pipe")
    rank = lax.axis_index("seq")
    sections = lax.axis_size("pipe")
    ranks = lax.axis_size("seq")
    z, xh, core = rank // 4, (rank // 2) % 2, rank % 2
    other = z * 4 + (1 - xh) * 2 + core
    place = z * 2 + core
    following = (section + 1) % sections
    before = (section + sections - 1) % sections
    ahead = (section + 2) % sections
    behind = (section + sections - 2) % sections
    odd = section % 2 == 1
    text_start = rows * ranks - TXT

    barrier = pltpu.get_barrier_semaphore()
    for step in range(1, ranks):
        pl.semaphore_signal(
            barrier, 1, device_id=(section, (rank + step) % ranks), device_id_type=MESH
        )
    for there in (following, before):
        for column in (rank, other):
            pl.semaphore_signal(barrier, 1, device_id=(there, column), device_id_type=MESH)
    for there in (ahead, behind):
        pl.semaphore_signal(barrier, 1, device_id=(there, rank), device_id_type=MESH)

    loads = [
        pltpu.make_async_copy(held_hbm.at[0], xin_ref.at[0], load_sem.at[0]),
        pltpu.make_async_copy(entering_hbm, xin_ref.at[1], load_sem.at[1]),
    ]
    for copy in loads:
        copy.start()
    weight_loads = {}
    for hop in HOPS:
        for cc in range(2):
            head = ((z + hop) % 4) * 4 + xh * 2 + (core + cc) % 2
            for third in range(3):
                copy = pltpu.make_async_copy(
                    wqkv_hbm.at[
                        0, :, pl.ds(pl.multiple_of(third * inner + head * HD, HD), HD)
                    ],
                    w_ref.at[hop, :, pl.ds((third * 2 + cc) * HD, HD)],
                    w_sem.at[hop, cc, third],
                )
                weight_loads.setdefault(hop, []).append(copy)
    wo_load = pltpu.make_async_copy(wout_hbm.at[0], wo_ref, wo_sem)

    def start_weights(index):
        if index < len(HOPS):
            for copy in weight_loads[HOPS[index]]:
                copy.start()

    start_weights(0)
    start_weights(1)

    for copy in loads:
        copy.wait()
    pl.semaphore_wait(barrier, ranks - 1 + 6)

    def cross_copy(index):
        if index < 2:
            lines = pl.ds(index * half, half)
            source, target = xin_ref.at[0, lines], xother_ref.at[0, lines]
        else:
            source, target = xin_ref.at[1], xother_ref.at[1]
        return pltpu.make_async_remote_copy(
            source,
            target,
            cross_send.at[index],
            cross_recv.at[index],
            device_id=(section, other),
            device_id_type=MESH,
        )

    cross_copy(0).start()
    cross_copy(1).start()

    @pl.when(section == 0)
    def _():
        cross_copy(2).start()

    kind_row = jnp.full((1, width), kind_ref[0], jnp.int32)

    def mod_row(index, column):
        text = (column >= text_start // rows).astype(jnp.int32)
        pick = (kind_row == 0) & (jnp.full((1, width), text, jnp.int32) == 1)
        return jnp.where(pick, mod_ref[index + 3], mod_ref[index])

    def mix(x, start, column):
        x = x.astype(jnp.float32)
        center = x - jnp.mean(x, axis=-1, keepdims=True)
        normed = center * lax.rsqrt(jnp.mean(center * center, axis=-1, keepdims=True) + EPS)
        mixed = normed * (1.0 + mod_row(1, column)) + mod_row(0, column)
        mixed_ref[start : start + x.shape[0]] = mixed.astype(jnp.bfloat16)

    chunks = (
        (0, slice(None), 0),
        (0, 0, 1),
        (0, 1, 1),
        (1, 0, slice(None)),
        (1, 1, slice(None)),
    )

    def pieces(chunk):
        return 1 if chunk in (1, 2) else 2

    def cut(ref, chunk):
        return ref.at[0] if pieces(chunk) == 1 else ref

    def exchange(chunk, hop, cc, keys):
        step, halves, column = chunks[chunk]
        target = ((z + hop) % 4) * 4 + xh * 2 + (core + cc) % 2
        if keys:
            source = cut(kvs_ref.at[chunk, hop, cc], chunk)
            there = kv_ref.at[step, place, halves, column]
            sems = kv_send, kv_recv
        else:
            source = cut(qs_ref.at[chunk, hop, cc], chunk)
            there = q_ref.at[step, halves, place, column]
            sems = q_send, q_recv
        return pltpu.make_async_remote_copy(
            source,
            there,
            sems[0].at[chunk, hop, cc],
            sems[1].at[chunk, hop, cc],
            device_id=(section, target),
            device_id_type=MESH,
        )

    def rms(values, gain):
        return (
            values
            * lax.rsqrt(jnp.mean(values * values, axis=-1, keepdims=True) + EPS)
            * gain
        ).astype(jnp.bfloat16)

    def project(chunk):
        step, halves, column = chunks[chunk]
        count = pieces(chunk)
        shape = (count, half, HD) if count == 2 else (half, HD)
        for index, hop in enumerate(HOPS):
            if chunk == 0:
                for copy in weight_loads[hop]:
                    copy.wait()
                start_weights(index + 2)
            product = jnp.dot(
                mixed_ref[0 : count * half], w_ref[hop], preferred_element_type=jnp.float32
            )
            for cc in range(2):
                query, key, value = (
                    product[:, (third * 2 + cc) * HD : (third * 2 + cc + 1) * HD]
                    for third in range(3)
                )
                query = rms(query, qg_ref[...]).reshape(shape)
                key = rms(key, kg_ref[...]).reshape(shape)
                value = value.astype(jnp.bfloat16).reshape(shape)
                if hop == 0 and cc == 0:
                    kv_ref[step, place, halves, column, :, 0:HD] = key
                    kv_ref[step, place, halves, column, :, HD : 2 * HD] = value
                    q_ref[step, halves, place, column] = query
                else:
                    first = slice(None) if count == 2 else 0
                    kvs_ref[chunk, hop, cc, first, :, 0:HD] = key
                    kvs_ref[chunk, hop, cc, first, :, HD : 2 * HD] = value
                    qs_ref[chunk, hop, cc, first] = query
                    exchange(chunk, hop, cc, True).start()

    pairs = [(hop, cc) for hop in (0, 3, 2, 1) for cc in range(2) if hop or cc]

    def send_queries(chunk):
        for hop, cc in pairs:
            exchange(chunk, hop, cc, False).start()

    def att_copy(step, n, column, cc):
        step_z = (n + n // 4) % 4
        at = n // 4
        ct = (core + cc) % 2
        return pltpu.make_async_remote_copy(
            atts_ref.at[step, n, ct, column],
            att_ref.at[
                step,
                pl.ds(pl.multiple_of(at * half, half), half),
                pl.ds(pl.multiple_of(rank * HD, HD), HD),
            ],
            att_send.at[step, at, step_z, column, cc],
            att_recv.at[step, at, step_z, column, cc],
            device_id=(
                section,
                ((z + step_z) % 4) * 4 + ((xh + column) % 2) * 2 + ct,
            ),
            device_id_type=MESH,
        )

    def finish(step, at):
        for n in range(4 * at, 4 * at + 4):
            for column in range(2):
                for cc in range(2):
                    if (n + n // 4) % 4 or column or cc:
                        att_copy(step, n, column, cc).wait_recv()
        gate = mod_row(2, rank)
        lines = slice(at * half, (at + 1) * half)
        tile = 512
        for n in range(width // tile):
            cols = slice(n * tile, (n + 1) * tile)
            update = jnp.dot(
                att_ref[step, lines], wo_ref[:, cols], preferred_element_type=jnp.float32
            )
            xsend_ref[step, lines, cols] = (
                xin_ref[step, lines, cols].astype(jnp.float32) + gate[:, cols] * update
            ).astype(jnp.bfloat16)
        for index in range(at * PARTS // 2, (at + 1) * PARTS // 2):
            if step == 1:
                pipe_copy(1, index).start()
            else:

                @pl.when(odd)
                def _():
                    relay_copy(index).start()

                @pl.when(jnp.logical_not(odd))
                def _():
                    pipe_copy(0, index).start()
                    side_copy(index).start()

    def part_of(index):
        return pl.ds(index * part, part)

    def pipe_copy(step, index):
        return pltpu.make_async_remote_copy(
            xsend_ref.at[step, part_of(index)],
            out_ref.at[step, part_of(index)],
            pipe_send.at[step, index],
            pipe_recv.at[step, index],
            device_id=(following, rank),
            device_id_type=MESH,
        )

    def side_copy(index):
        return pltpu.make_async_remote_copy(
            xsend_ref.at[0, part_of(index)],
            xother_ref.at[1, part_of(index)],
            pipe_send.at[2, index],
            pipe_recv.at[2, index],
            device_id=(following, other),
            device_id_type=MESH,
        )

    def relay_copy(index):
        return pltpu.make_async_remote_copy(
            xsend_ref.at[0, part_of(index)],
            relay_ref.at[part_of(index)],
            pipe_send.at[0, index],
            relay_recv.at[index],
            device_id=(ahead, rank),
            device_id_type=MESH,
        )

    def forward_copy(index, which):
        return pltpu.make_async_remote_copy(
            relay_ref.at[part_of(index)],
            (out_ref.at[0] if which == 0 else xother_ref.at[1]).at[part_of(index)],
            relay_send.at[which, index],
            pipe_recv.at[2 * which, index],
            device_id=(before, rank if which == 0 else other),
            device_id_type=MESH,
        )

    def attend(step, live):
        for chunk in range(5):
            if chunks[chunk][0] == step:
                for hop, cc in pairs:
                    exchange(chunk, hop, cc, True).wait_recv()
        spot = lax.broadcasted_iota(jnp.int32, (1, 4 * rows), 1)
        column = (xh + (spot // half) % 2) % 2
        key_rank = 12 + column * 2 + spot // (2 * rows)
        position = key_rank * rows + ((spot // rows) % 2) * half + spot % half
        limit = jnp.full((1, 4 * rows), text_start + live, jnp.int32)
        bias = jnp.where(position < limit, 0.0, -1e30).astype(jnp.float32)
        clear = (ranks - 4) * rows

        def pair(i, carry):
            @pl.when(i == 3)
            def _():
                if step == 0:
                    wo_load.wait()
                finish(step, 0)

            scores = []
            for u in range(2):
                n = 2 * i + u
                at = n // 4
                step_z = (n + at) % 4
                hop = (4 - step_z) % 4
                for cc in range(2):
                    for chunk in range(5):
                        if chunks[chunk][0] == step:
                            if step == 0:
                                due = at == 0
                            else:
                                due = at == chunk - 3
                            if cc == 0:
                                due = due & (step_z > 0)

                            @pl.when(due)
                            def _():
                                exchange(chunk, hop, cc, False).wait_recv()

                zt = (z + step_z) % 4
                query = q_ref[step, at, pl.ds(2 * zt, 2)].reshape(2 * rows, HD)
                keys = kv_ref[step, :, :, :, :, 0:HD].reshape(ranks * rows, HD)
                scores.append(
                    lax.dot_general(
                        query,
                        keys,
                        (((1,), (1,)), ((), ())),
                        preferred_element_type=jnp.float32,
                    )
                )
            for u in range(2):
                n = 2 * i + u
                at = n // 4
                step_z = (n + at) % 4
                score = jnp.concatenate(
                    [scores[u][:, :clear], scores[u][:, clear:] + bias], axis=1
                )
                top = jnp.max(score, axis=-1, keepdims=True)
                weights = jnp.exp2((score - top) * (HD ** (-0.5) * LOG2E))
                denom = jnp.sum(weights, axis=-1, keepdims=True)
                values = kv_ref[step, :, :, :, :, HD : 2 * HD].reshape(ranks * rows, HD)
                summed = jnp.dot(
                    weights.astype(jnp.bfloat16), values, preferred_element_type=jnp.float32
                )
                atts_ref[step, n] = (
                    (summed / denom).astype(jnp.bfloat16).reshape(2, 2, half, HD)
                )

                @pl.when(step_z > 0)
                def _():
                    att_copy(step, n, 0, 0).start()

                @pl.when(step_z == 0)
                def _():
                    att_ref[
                        step,
                        pl.ds(pl.multiple_of(at * half, half), half),
                        pl.ds(pl.multiple_of(rank * HD, HD), HD),
                    ] = atts_ref[step, n, core, 0]

                att_copy(step, n, 0, 1).start()
                att_copy(step, n, 1, 0).start()
                att_copy(step, n, 1, 1).start()
            return carry

        lax.fori_loop(0, 4, pair, 0)
        finish(step, 1)

    mix(xin_ref[0], 0, rank)
    project(0)
    send_queries(0)
    wo_load.start()
    for at in range(2):
        cross_copy(at).wait_recv()
        mix(xother_ref[0, at * half : (at + 1) * half], 0, other)
        project(1 + at)
    send_queries(1)
    send_queries(2)
    attend(0, counts_ref[section])

    @pl.when(odd)
    def _():
        for index in range(PARTS):
            relay_copy(index).wait_recv()
            forward_copy(index, 0).start()

            @pl.when(section != 1)
            def _():
                forward_copy(index, 1).start()

    for at in range(2):
        lines = slice(at * half, (at + 1) * half)
        for index in range(at * PARTS // 2, (at + 1) * PARTS // 2):
            pipe_copy(0, index).wait_recv()

        @pl.when(section > 0)
        def _():
            xin_ref[1, lines] = out_ref[0, lines]
            for index in range(at * PARTS // 2, (at + 1) * PARTS // 2):
                side_copy(index).wait_recv()

        if at == 0:

            @pl.when(section == 0)
            def _():
                cross_copy(2).wait_recv()

        mix(xin_ref[1, lines], 0, rank)
        mix(xother_ref[1, lines], half, other)
        project(3 + at)
    send_queries(3)
    send_queries(4)
    attend(1, counts_ref[(section + sections) % (sections + 1)])

    cross_copy(0).wait_send()
    cross_copy(1).wait_send()

    @pl.when(section == 0)
    def _():
        cross_copy(2).wait_send()

    @pl.when(jnp.logical_not(odd))
    def _():
        for index in range(PARTS):
            side_copy(index).wait_send()

    @pl.when(odd)
    def _():
        for index in range(PARTS):
            forward_copy(index, 0).wait_send()

            @pl.when(section != 1)
            def _():
                forward_copy(index, 1).wait_send()

    for index in range(PARTS):
        pipe_copy(0, index).wait_send()
    for chunk in range(5):
        for hop, cc in pairs:
            exchange(chunk, hop, cc, True).wait_send()
            exchange(chunk, hop, cc, False).wait_send()
    for step in range(2):
        for n in range(8):
            for column in range(2):
                for cc in range(2):
                    if (n + n // 4) % 4 or column or cc:
                        att_copy(step, n, column, cc).wait_send()
    for index in range(PARTS):
        pipe_copy(1, index).wait()


def shards(held, entering, counts, kind, modulation, w_qkv, w_out, q_gain, k_gain):
    rows, width = entering.shape
    half = rows // 2
    inner = w_out.shape[1]
    bf16 = jnp.bfloat16
    vmem = pl.BlockSpec(memory_space=pltpu.VMEM)
    smem = pl.BlockSpec(memory_space=pltpu.SMEM)
    hbm = pl.BlockSpec(memory_space=pl.ANY)
    dma = pltpu.SemaphoreType.DMA
    out = pl.pallas_call(
        body,
        out_shape=jax.ShapeDtypeStruct((2, rows, width), bf16),
        in_specs=[smem, smem, hbm, hbm, vmem, hbm, hbm, vmem, vmem],
        out_specs=vmem,
        scratch_shapes=[
            pltpu.VMEM((4, width, 6 * HD), bf16),
            pltpu.VMEM((inner, width), bf16),
            pltpu.VMEM((2, rows, width), bf16),
            pltpu.VMEM((2, rows, width), bf16),
            pltpu.VMEM((2, rows, width), bf16),
            pltpu.VMEM((rows, width), bf16),
            pltpu.VMEM((rows, width), bf16),
            pltpu.VMEM((2, 8, 2, 2, half, 2 * HD), bf16),
            pltpu.VMEM((2, 2, 8, 2, half, HD), bf16),
            pltpu.VMEM((5, 4, 2, 2, half, 2 * HD), bf16),
            pltpu.VMEM((5, 4, 2, 2, half, HD), bf16),
            pltpu.VMEM((2, rows, inner), bf16),
            pltpu.VMEM((2, 8, 2, 2, half, HD), bf16),
            dma((2,)),
            dma((4, 2, 3)),
            dma,
            dma((3,)),
            dma((3,)),
            dma((5, 4, 2)),
            dma((5, 4, 2)),
            dma((5, 4, 2)),
            dma((5, 4, 2)),
            dma((2, 2, 4, 2, 2)),
            dma((2, 2, 4, 2, 2)),
            dma((3, PARTS)),
            dma((3, PARTS)),
            dma((PARTS,)),
            dma((2, PARTS)),
        ],
        compiler_params=pltpu.CompilerParams(
            collective_id=0, has_side_effects=True, vmem_limit_bytes=60 * 1024 * 1024
        ),
        name="relay",
    )(counts, kind, held, entering, modulation.transpose(1, 0, 2), w_qkv, w_out, q_gain, k_gain)
    return out[:, None]


def solution(mesh):
    placed = (
        P("pipe", "seq", None),
        P("seq", None),
        P(),
        P("pipe"),
        P("pipe", None, None),
        P("pipe", None, None),
        P("pipe", None, None),
        P("pipe", None),
        P("pipe", None),
    )
    return jax.shard_map(
        shards, mesh=mesh, in_specs=placed, out_specs=P(None, "pipe", "seq", None), check_vma=False
    )
```

```python
import functools

import jax
import jax.numpy as jnp
from jax import lax
from jax.experimental import pallas as pl
from jax.experimental.pallas import tpu as pltpu
from jax.sharding import PartitionSpec as P

HD = 128
TXT = 256
EPS = 1e-06
MESH = pl.DeviceIdType.MESH
LOG2E = 1.4426950408889634

HOPS = (2, 1, 3, 0)
PARTS = 4


def body(
    counts_ref,
    kind_ref,
    held_hbm,
    entering_hbm,
    mod_ref,
    wqkv_hbm,
    wout_hbm,
    qg_ref,
    kg_ref,
    out_ref,
    w_ref,
    wo_ref,
    xin_ref,
    xother_ref,
    xsend_ref,
    relay_ref,
    mixed_ref,
    kv_ref,
    q_ref,
    kvs_ref,
    qs_ref,
    att_ref,
    atts_ref,
    load_sem,
    w_sem,
    wo_sem,
    cross_send,
    cross_recv,
    kv_send,
    kv_recv,
    q_send,
    q_recv,
    att_send,
    att_recv,
    pipe_send,
    pipe_recv,
    relay_recv,
    relay_send,
):
    rows, width = xin_ref.shape[1], xin_ref.shape[2]
    half = rows // 2
    part = rows // PARTS
    inner = wo_ref.shape[0]
    section = lax.axis_index("pipe")
    rank = lax.axis_index("seq")
    sections = lax.axis_size("pipe")
    ranks = lax.axis_size("seq")
    z, xh, core = rank // 4, (rank // 2) % 2, rank % 2
    other = z * 4 + (1 - xh) * 2 + core
    place = z * 2 + core
    following = (section + 1) % sections
    before = (section + sections - 1) % sections
    ahead = (section + 2) % sections
    behind = (section + sections - 2) % sections
    odd = section % 2 == 1
    text_start = rows * ranks - TXT

    barrier = pltpu.get_barrier_semaphore()
    for step in range(1, ranks):
        pl.semaphore_signal(
            barrier, 1, device_id=(section, (rank + step) % ranks), device_id_type=MESH
        )
    for there in (following, before):
        for column in (rank, other):
            pl.semaphore_signal(barrier, 1, device_id=(there, column), device_id_type=MESH)
    for there in (ahead, behind):
        pl.semaphore_signal(barrier, 1, device_id=(there, rank), device_id_type=MESH)

    loads = [
        pltpu.make_async_copy(held_hbm.at[0], xin_ref.at[0], load_sem.at[0]),
        pltpu.make_async_copy(entering_hbm, xin_ref.at[1], load_sem.at[1]),
    ]
    for copy in loads:
        copy.start()
    weight_loads = {}
    for hop in HOPS:
        for cc in range(2):
            head = ((z + hop) % 4) * 4 + xh * 2 + (core + cc) % 2
            for third in range(3):
                copy = pltpu.make_async_copy(
                    wqkv_hbm.at[
                        0, :, pl.ds(pl.multiple_of(third * inner + head * HD, HD), HD)
                    ],
                    w_ref.at[hop, :, pl.ds((third * 2 + cc) * HD, HD)],
                    w_sem.at[hop, cc, third],
                )
                weight_loads.setdefault(hop, []).append(copy)
    wo_load = pltpu.make_async_copy(wout_hbm.at[0], wo_ref, wo_sem)

    def start_weights(index):
        if index < len(HOPS):
            for copy in weight_loads[HOPS[index]]:
                copy.start()

    start_weights(0)
    start_weights(1)

    for copy in loads:
        copy.wait()
    pl.semaphore_wait(barrier, ranks - 1 + 6)

    def cross_copy(index):
        if index < 2:
            lines = pl.ds(index * half, half)
            source, target = xin_ref.at[0, lines], xother_ref.at[0, lines]
        else:
            source, target = xin_ref.at[1], xother_ref.at[1]
        return pltpu.make_async_remote_copy(
            source,
            target,
            cross_send.at[index],
            cross_recv.at[index],
            device_id=(section, other),
            device_id_type=MESH,
        )

    cross_copy(0).start()
    cross_copy(1).start()

    @pl.when(section == 0)
    def _():
        cross_copy(2).start()

    kind_row = jnp.full((1, width), kind_ref[0], jnp.int32)

    def mod_row(index, column):
        text = (column >= text_start // rows).astype(jnp.int32)
        pick = (kind_row == 0) & (jnp.full((1, width), text, jnp.int32) == 1)
        return jnp.where(pick, mod_ref[index + 3], mod_ref[index])

    def mix(x, start, column):
        x = x.astype(jnp.float32)
        center = x - jnp.mean(x, axis=-1, keepdims=True)
        normed = center * lax.rsqrt(jnp.mean(center * center, axis=-1, keepdims=True) + EPS)
        mixed = normed * (1.0 + mod_row(1, column)) + mod_row(0, column)
        mixed_ref[start : start + x.shape[0]] = mixed.astype(jnp.bfloat16)

    chunks = (
        (0, slice(None), 0),
        (0, 0, 1),
        (0, 1, 1),
        (1, 0, slice(None)),
        (1, 1, slice(None)),
    )

    def pieces(chunk):
        return 1 if chunk in (1, 2) else 2

    def cut(ref, chunk):
        return ref.at[0] if pieces(chunk) == 1 else ref

    def exchange(chunk, hop, cc, keys):
        step, halves, column = chunks[chunk]
        target = ((z + hop) % 4) * 4 + xh * 2 + (core + cc) % 2
        if keys:
            source = cut(kvs_ref.at[chunk, hop, cc], chunk)
            there = kv_ref.at[step, place, halves, column]
            sems = kv_send, kv_recv
        else:
            source = cut(qs_ref.at[chunk, hop, cc], chunk)
            there = q_ref.at[step, halves, place, column]
            sems = q_send, q_recv
        return pltpu.make_async_remote_copy(
            source,
            there,
            sems[0].at[chunk, hop, cc],
            sems[1].at[chunk, hop, cc],
            device_id=(section, target),
            device_id_type=MESH,
        )

    def rms(values, gain):
        return (
            values
            * lax.rsqrt(jnp.mean(values * values, axis=-1, keepdims=True) + EPS)
            * gain
        ).astype(jnp.bfloat16)

    def project(chunk):
        step, halves, column = chunks[chunk]
        count = pieces(chunk)
        shape = (count, half, HD) if count == 2 else (half, HD)
        for index, hop in enumerate(HOPS):
            if chunk == 0:
                for copy in weight_loads[hop]:
                    copy.wait()
                start_weights(index + 2)
            product = jnp.dot(
                mixed_ref[0 : count * half], w_ref[hop], preferred_element_type=jnp.float32
            )
            for cc in range(2):
                query, key, value = (
                    product[:, (third * 2 + cc) * HD : (third * 2 + cc + 1) * HD]
                    for third in range(3)
                )
                query = rms(query, qg_ref[...]).reshape(shape)
                key = rms(key, kg_ref[...]).reshape(shape)
                value = value.astype(jnp.bfloat16).reshape(shape)
                if hop == 0 and cc == 0:
                    kv_ref[step, place, halves, column, :, 0:HD] = key
                    kv_ref[step, place, halves, column, :, HD : 2 * HD] = value
                    q_ref[step, halves, place, column] = query
                else:
                    first = slice(None) if count == 2 else 0
                    kvs_ref[chunk, hop, cc, first, :, 0:HD] = key
                    kvs_ref[chunk, hop, cc, first, :, HD : 2 * HD] = value
                    qs_ref[chunk, hop, cc, first] = query
                    exchange(chunk, hop, cc, True).start()

    pairs = [(hop, cc) for hop in (0, 3, 2, 1) for cc in range(2) if hop or cc]

    def send_queries(chunk):
        for hop, cc in pairs:
            exchange(chunk, hop, cc, False).start()

    def att_copy(step, n, column, cc):
        step_z = (n + n // 4) % 4
        at = n // 4
        ct = (core + cc) % 2
        return pltpu.make_async_remote_copy(
            atts_ref.at[step, n, ct, column],
            att_ref.at[
                step,
                pl.ds(pl.multiple_of(at * half, half), half),
                pl.ds(pl.multiple_of(rank * HD, HD), HD),
            ],
            att_send.at[step, at, step_z, column, cc],
            att_recv.at[step, at, step_z, column, cc],
            device_id=(
                section,
                ((z + step_z) % 4) * 4 + ((xh + column) % 2) * 2 + ct,
            ),
            device_id_type=MESH,
        )

    def finish(step, at):
        for n in range(4 * at, 4 * at + 4):
            for column in range(2):
                for cc in range(2):
                    if (n + n // 4) % 4 or column or cc:
                        att_copy(step, n, column, cc).wait_recv()
        if step == 0 and at == 1:
            forward(0, 1)
        gate = mod_row(2, rank)
        lines = slice(at * half, (at + 1) * half)
        tile = 512
        for n in range(width // tile):
            cols = slice(n * tile, (n + 1) * tile)
            update = jnp.dot(
                att_ref[step, lines], wo_ref[:, cols], preferred_element_type=jnp.float32
            )
            xsend_ref[step, lines, cols] = (
                xin_ref[step, lines, cols].astype(jnp.float32) + gate[:, cols] * update
            ).astype(jnp.bfloat16)
        for index in range(at * PARTS // 2, (at + 1) * PARTS // 2):
            if step == 1:
                pipe_copy(1, index).start()
            else:

                @pl.when(odd)
                def _():
                    relay_copy(index).start()

                @pl.when(jnp.logical_not(odd))
                def _():
                    pipe_copy(0, index).start()
                    side_copy(index).start()

    def part_of(index):
        return pl.ds(index * part, part)

    def pipe_copy(step, index):
        return pltpu.make_async_remote_copy(
            xsend_ref.at[step, part_of(index)],
            out_ref.at[step, part_of(index)],
            pipe_send.at[step, index],
            pipe_recv.at[step, index],
            device_id=(following, rank),
            device_id_type=MESH,
        )

    def side_copy(index):
        return pltpu.make_async_remote_copy(
            xsend_ref.at[0, part_of(index)],
            xother_ref.at[1, part_of(index)],
            pipe_send.at[2, index],
            pipe_recv.at[2, index],
            device_id=(following, other),
            device_id_type=MESH,
        )

    def relay_copy(index):
        return pltpu.make_async_remote_copy(
            xsend_ref.at[0, part_of(index)],
            relay_ref.at[part_of(index)],
            pipe_send.at[0, index],
            relay_recv.at[index],
            device_id=(ahead, rank),
            device_id_type=MESH,
        )

    def forward_copy(index, which):
        return pltpu.make_async_remote_copy(
            relay_ref.at[part_of(index)],
            (out_ref.at[0] if which == 0 else xother_ref.at[1]).at[part_of(index)],
            relay_send.at[which, index],
            pipe_recv.at[2 * which, index],
            device_id=(before, rank if which == 0 else other),
            device_id_type=MESH,
        )

    def forward(first, last):
        @pl.when(odd)
        def _():
            for index in range(first, last):
                relay_copy(index).wait_recv()
                forward_copy(index, 0).start()

                @pl.when(section != 1)
                def _():
                    forward_copy(index, 1).start()

    def attend(step, live):
        for chunk in range(5):
            if chunks[chunk][0] == step:
                for hop, cc in pairs:
                    exchange(chunk, hop, cc, True).wait_recv()
        spot = lax.broadcasted_iota(jnp.int32, (1, 4 * rows), 1)
        column = (xh + (spot // half) % 2) % 2
        key_rank = 12 + column * 2 + spot // (2 * rows)
        position = key_rank * rows + ((spot // rows) % 2) * half + spot % half
        limit = jnp.full((1, 4 * rows), text_start + live, jnp.int32)
        bias = jnp.where(position < limit, 0.0, -1e30).astype(jnp.float32)
        clear = (ranks - 4) * rows

        def pair(i, carry):
            @pl.when(i == 2 + step)
            def _():
                if step == 0:
                    wo_load.wait()
                finish(step, 0)

            scores = []
            for u in range(2):
                n = 2 * i + u
                at = n // 4
                step_z = (n + at) % 4
                hop = (4 - step_z) % 4
                for cc in range(2):
                    for chunk in range(5):
                        if chunks[chunk][0] == step:
                            if step == 0:
                                due = at == 0
                            else:
                                due = at == chunk - 3
                            if cc == 0:
                                due = due & (step_z > 0)

                            @pl.when(due)
                            def _():
                                exchange(chunk, hop, cc, False).wait_recv()

                zt = (z + step_z) % 4
                query = q_ref[step, at, pl.ds(2 * zt, 2)].reshape(2 * rows, HD)
                keys = kv_ref[step, :, :, :, :, 0:HD].reshape(ranks * rows, HD)
                scores.append(
                    lax.dot_general(
                        query,
                        keys,
                        (((1,), (1,)), ((), ())),
                        preferred_element_type=jnp.float32,
                    )
                )
            for u in range(2):
                n = 2 * i + u
                at = n // 4
                step_z = (n + at) % 4
                score = jnp.concatenate(
                    [scores[u][:, :clear], scores[u][:, clear:] + bias], axis=1
                )
                top = jnp.max(score, axis=-1, keepdims=True)
                weights = jnp.exp2((score - top) * (HD ** (-0.5) * LOG2E))
                denom = jnp.sum(weights, axis=-1, keepdims=True)
                values = kv_ref[step, :, :, :, :, HD : 2 * HD].reshape(ranks * rows, HD)
                summed = jnp.dot(
                    weights.astype(jnp.bfloat16), values, preferred_element_type=jnp.float32
                )
                atts_ref[step, n] = (
                    (summed / denom).astype(jnp.bfloat16).reshape(2, 2, half, HD)
                )

                @pl.when(step_z > 0)
                def _():
                    att_copy(step, n, 0, 0).start()

                @pl.when(step_z == 0)
                def _():
                    att_ref[
                        step,
                        pl.ds(pl.multiple_of(at * half, half), half),
                        pl.ds(pl.multiple_of(rank * HD, HD), HD),
                    ] = atts_ref[step, n, core, 0]

                att_copy(step, n, 0, 1).start()
                att_copy(step, n, 1, 0).start()
                att_copy(step, n, 1, 1).start()
            return carry

        lax.fori_loop(0, 4, pair, 0)
        finish(step, 1)

    mix(xin_ref[0], 0, rank)
    project(0)
    send_queries(0)
    wo_load.start()
    for at in range(2):
        cross_copy(at).wait_recv()
        mix(xother_ref[0, at * half : (at + 1) * half], 0, other)
        project(1 + at)
    send_queries(1)
    send_queries(2)
    attend(0, counts_ref[section])

    for at in range(2):
        lines = slice(at * half, (at + 1) * half)
        forward(max(1, at * PARTS // 2), (at + 1) * PARTS // 2)
        for index in range(at * PARTS // 2, (at + 1) * PARTS // 2):
            pipe_copy(0, index).wait_recv()

        @pl.when(section > 0)
        def _():
            xin_ref[1, lines] = out_ref[0, lines]
            for index in range(at * PARTS // 2, (at + 1) * PARTS // 2):
                side_copy(index).wait_recv()

        if at == 0:

            @pl.when(section == 0)
            def _():
                cross_copy(2).wait_recv()

        mix(xin_ref[1, lines], 0, rank)
        mix(xother_ref[1, lines], half, other)
        project(3 + at)
    send_queries(3)
    send_queries(4)
    attend(1, counts_ref[(section + sections) % (sections + 1)])

    cross_copy(0).wait_send()
    cross_copy(1).wait_send()

    @pl.when(section == 0)
    def _():
        cross_copy(2).wait_send()

    @pl.when(jnp.logical_not(odd))
    def _():
        for index in range(PARTS):
            side_copy(index).wait_send()

    @pl.when(odd)
    def _():
        for index in range(PARTS):
            forward_copy(index, 0).wait_send()

            @pl.when(section != 1)
            def _():
                forward_copy(index, 1).wait_send()

    for index in range(PARTS):
        pipe_copy(0, index).wait_send()
    for chunk in range(5):
        for hop, cc in pairs:
            exchange(chunk, hop, cc, True).wait_send()
            exchange(chunk, hop, cc, False).wait_send()
    for step in range(2):
        for n in range(8):
            for column in range(2):
                for cc in range(2):
                    if (n + n // 4) % 4 or column or cc:
                        att_copy(step, n, column, cc).wait_send()
    for index in range(PARTS):
        pipe_copy(1, index).wait()


def shards(held, entering, counts, kind, modulation, w_qkv, w_out, q_gain, k_gain):
    rows, width = entering.shape
    half = rows // 2
    inner = w_out.shape[1]
    bf16 = jnp.bfloat16
    vmem = pl.BlockSpec(memory_space=pltpu.VMEM)
    smem = pl.BlockSpec(memory_space=pltpu.SMEM)
    hbm = pl.BlockSpec(memory_space=pl.ANY)
    dma = pltpu.SemaphoreType.DMA
    out = pl.pallas_call(
        body,
        out_shape=jax.ShapeDtypeStruct((2, rows, width), bf16),
        in_specs=[smem, smem, hbm, hbm, vmem, hbm, hbm, vmem, vmem],
        out_specs=vmem,
        scratch_shapes=[
            pltpu.VMEM((4, width, 6 * HD), bf16),
            pltpu.VMEM((inner, width), bf16),
            pltpu.VMEM((2, rows, width), bf16),
            pltpu.VMEM((2, rows, width), bf16),
            pltpu.VMEM((2, rows, width), bf16),
            pltpu.VMEM((rows, width), bf16),
            pltpu.VMEM((rows, width), bf16),
            pltpu.VMEM((2, 8, 2, 2, half, 2 * HD), bf16),
            pltpu.VMEM((2, 2, 8, 2, half, HD), bf16),
            pltpu.VMEM((5, 4, 2, 2, half, 2 * HD), bf16),
            pltpu.VMEM((5, 4, 2, 2, half, HD), bf16),
            pltpu.VMEM((2, rows, inner), bf16),
            pltpu.VMEM((2, 8, 2, 2, half, HD), bf16),
            dma((2,)),
            dma((4, 2, 3)),
            dma,
            dma((3,)),
            dma((3,)),
            dma((5, 4, 2)),
            dma((5, 4, 2)),
            dma((5, 4, 2)),
            dma((5, 4, 2)),
            dma((2, 2, 4, 2, 2)),
            dma((2, 2, 4, 2, 2)),
            dma((3, PARTS)),
            dma((3, PARTS)),
            dma((PARTS,)),
            dma((2, PARTS)),
        ],
        compiler_params=pltpu.CompilerParams(
            collective_id=0, has_side_effects=True, vmem_limit_bytes=60 * 1024 * 1024
        ),
        name="relay",
    )(counts, kind, held, entering, modulation.transpose(1, 0, 2), w_qkv, w_out, q_gain, k_gain)
    return out[:, None]


def solution(mesh):
    placed = (
        P("pipe", "seq", None),
        P("seq", None),
        P(),
        P("pipe"),
        P("pipe", None, None),
        P("pipe", None, None),
        P("pipe", None, None),
        P("pipe", None),
        P("pipe", None),
    )
    return jax.shard_map(
        shards, mesh=mesh, in_specs=placed, out_specs=P(None, "pipe", "seq", None), check_vma=False
    )
```
